32 devices in a mesh: segment: 2 (over x), seq: 4 (over y, core), head: 4 (over z).
Axes of the slice: x: 2, y: 2, z: 4, core: 2. Of those that a mesh axis runs over, the one named last changes fastest.
Arguments:
- stream: bfloat16 [2, 512, 4096], P(None, 'seq', 'head'), may hold values from -6 to 6
- in_gain: float32 [2, 4096], P('segment'), may hold values from 0.25 to 1.75
- w_qkv: bfloat16 [2, 4096, 4, 3, 512], P('segment', None, 'head'), may hold values from -0.09375 to 0.09375
- qk_gain: float32 [2, 4, 2, 512], P('segment', 'head'), may hold values from 0.25 to 1.75
- w_one: bfloat16 [2, 4, 512, 768], P('segment', 'head'), may hold values from -0.25 to 0.25
- w_three: bfloat16 [2, 4, 512, 768], P('segment', 'head'), may hold values from -0.25 to 0.25
- w_two: bfloat16 [2, 4, 768, 512], P('segment', 'head'), may hold values from -0.21875 to 0.21875
- token_rate: float32 [2, 2, 512], P('segment', None, 'seq'), may hold values from 0.05 to 1
- out_gain: float32 [2, 4, 512], P('segment', 'head'), may hold values from 0.25 to 1.75
- w_out: bfloat16 [2, 4, 512, 4096], P('segment', 'head'), may hold values from -0.125 to 0.125
Outputs:
- sections_out: bfloat16 [2, 2, 512, 4096], P('segment', None, 'seq', 'head')
The draws below stay inside these ranges and needn't reach their ends.
All inputs are finite; a program needn't handle non-finite values.
Results may differ from the reference program's by a relative error of at most 0.038.
Values may be sent and summed in bfloat16 or wider, within the bound.
A program may use at most 128 MiB of HBM per device.

```python
import math
import jax
import jax.numpy as jnp
from jax import lax

DH = 512
FF = 768
HEADS = 4
DM = 4096
SECTIONS = 2
SPANS = 2
NS_STEPS = 2
TOKENS = 512
N_SEQ = 4


def block_levels(stream_key, dims, split, least, high):
    gain = 1.0
    for axis_at, blocks in split:
        steps = jax.random.uniform(jax.random.fold_in(jax.random.fold_in(stream_key, 6), axis_at), (blocks,), jnp.float32, least / len(split), high / len(split))
        gain = gain * jnp.repeat(jnp.exp(steps), dims[axis_at] // blocks).reshape((-1,) + (1,) * (len(dims) - 1 - axis_at))
    return gain


def gaussian(own_key, shape, spread, limit, pieces=(), held_as=jnp.bfloat16):
    entries = jax.random.normal(own_key, shape, jnp.float32) * spread
    if len(pieces) > 0:
        entries = block_levels(own_key, shape, pieces, -0.22, 0.18) * entries
    return jnp.clip(entries, min=-limit, max=limit).astype(held_as)


def setup_inputs(seed: int = 0) -> dict:
    keys = jax.random.split(jax.random.key(seed), 11)
    stream = gaussian(keys[0], (SPANS, TOKENS, DM), 1.0, 6.0, ((1, 4), (2, 4)))
    in_gain = jnp.clip(1.0 + 0.15 * jax.random.normal(keys[1], (SECTIONS, DM), jnp.float32), 0.25, 1.75)
    w_qkv = gaussian(keys[2], (SECTIONS, DM, HEADS, 3, DH), DM ** -0.5, 0.09375, ((0, 2), (2, 4)))
    qk_gain = jnp.clip(1.0 + 0.15 * jax.random.normal(keys[3], (SECTIONS, HEADS, 2, DH), jnp.float32), 0.25, 1.75)
    w_one = gaussian(keys[4], (SECTIONS, HEADS, DH, FF), DH ** -0.5, 0.25, ((0, 2), (1, 4)))
    w_three = gaussian(keys[5], (SECTIONS, HEADS, DH, FF), DH ** -0.5, 0.25, ((0, 2), (1, 4)))
    w_two = gaussian(keys[6], (SECTIONS, HEADS, FF, DH), FF ** -0.5, 0.21875, ((0, 2), (1, 4)))
    token_rate = jnp.clip(jnp.exp(math.log(1.0) - 2.9957323 * jax.random.uniform(keys[7], (SECTIONS, SPANS, TOKENS), jnp.float32) ** block_levels(keys[7], (SECTIONS, SPANS, TOKENS), ((0, 2), (2, 4)), -0.2, 0.2)), 0.05, 1.0)
    out_gain = jnp.clip(1.0 + 0.15 * jax.random.normal(keys[8], (SECTIONS, HEADS, DH), jnp.float32), 0.25, 1.75)
    w_out = gaussian(keys[9], (SECTIONS, HEADS, DH, DM), (HEADS * DH) ** -0.5, 0.125, ((0, 2), (1, 4)))
    return dict(stream=stream, in_gain=in_gain, w_qkv=w_qkv, qk_gain=qk_gain, w_one=w_one, w_three=w_three, w_two=w_two, token_rate=token_rate, out_gain=out_gain, w_out=w_out)


ns_first = 3.4445
ns_second = -4.775
ns_third = 2.0315
update_step = 1.0
norm_eps = 1e-06
grad_eps = 1e-07

def rms_scale(values):
    return values * lax.rsqrt(lax.optimization_barrier(jnp.mean(values * values, axis=-1, keepdims=True)) + norm_eps)

def orthogonalize(gradient):
    current = (gradient / (jnp.sqrt(jnp.sum(gradient * gradient)) + grad_eps)).astype(jnp.bfloat16)
    row_count = gradient.shape[0]
    column_count = gradient.shape[1]
    for sweep_index in range(NS_STEPS):
        blocks = current.astype(jnp.float32).reshape(row_count, N_SEQ, column_count // N_SEQ)
        partial_grams = jnp.einsum('inb,jnb->nij', blocks, blocks).astype(jnp.bfloat16)
        gram_matrix = lax.optimization_barrier(jnp.sum(partial_grams.astype(jnp.float32), axis=0)).astype(jnp.bfloat16)
        square = jnp.dot(gram_matrix, gram_matrix, preferred_element_type=jnp.float32)
        mixing = (ns_second * gram_matrix.astype(jnp.float32) + ns_third * square).astype(jnp.bfloat16)
        current = (ns_first * current.astype(jnp.float32) + jnp.dot(mixing, current, preferred_element_type=jnp.float32)).astype(jnp.bfloat16)
    return current

def renormalize(weights, target_norms):
    return weights * (target_norms / (jnp.sqrt(lax.optimization_barrier(jnp.sum(weights * weights, axis=0))) + norm_eps))

def head_update(queries, key_rows, out_grad, fast, initial_norms):
    gate_fast, up_fast, down_fast = fast
    gate_low = gate_fast.astype(jnp.bfloat16)
    up_low = up_fast.astype(jnp.bfloat16)
    down_low = down_fast.astype(jnp.bfloat16)
    pre_gate = jnp.dot(key_rows, gate_low, preferred_element_type=jnp.float32)
    pre_up = jnp.dot(key_rows, up_low, preferred_element_type=jnp.float32)
    sigmoid_gate = jax.nn.sigmoid(pre_gate)
    gated = pre_gate * sigmoid_gate
    hidden = (gated * pre_up).astype(jnp.bfloat16)
    backward = jnp.dot(out_grad, down_low.T, preferred_element_type=jnp.float32)
    grad_gate = (backward * pre_up * sigmoid_gate * (1.0 + pre_gate * (1.0 - sigmoid_gate))).astype(jnp.bfloat16)
    grad_up = (backward * gated).astype(jnp.bfloat16)
    grad_first = jnp.dot(key_rows.T, grad_gate, preferred_element_type=jnp.float32)
    grad_third = jnp.dot(key_rows.T, grad_up, preferred_element_type=jnp.float32)
    grad_second = jnp.dot(out_grad.T, hidden, preferred_element_type=jnp.float32)
    gate_fast = renormalize(gate_fast - update_step * orthogonalize(grad_first).astype(jnp.float32), initial_norms[0])
    up_fast = renormalize(up_fast - update_step * orthogonalize(grad_third).astype(jnp.float32), initial_norms[1])
    down_fast = renormalize(down_fast - update_step * orthogonalize(grad_second).astype(jnp.float32).T, initial_norms[2])
    gate_out = jnp.dot(queries, gate_fast, precision=lax.Precision.HIGHEST)
    up_out = jnp.dot(queries, up_fast, precision=lax.Precision.HIGHEST)
    output = jnp.dot(jax.nn.silu(gate_out) * up_out, down_fast, precision=lax.Precision.HIGHEST)
    return (output, (gate_fast, up_fast, down_fast))

def run_section(residual, gain_row, qkv_weights, qk_gains, rate_row, out_gains, out_weights, fasts, norms):
    values = residual.astype(jnp.float32)
    normed = (rms_scale(values) * gain_row).astype(jnp.bfloat16)
    projected = jnp.dot(normed, qkv_weights.reshape(DM, HEADS * 3 * DH), preferred_element_type=jnp.float32)
    projected = projected.reshape(TOKENS, HEADS, 3, DH)
    mixed = jnp.zeros((TOKENS, DM), jnp.float32)
    new_fasts = []
    for head_index in range(HEADS):
        queries = rms_scale(projected[:, head_index, 0]) * qk_gains[head_index, 0]
        key_rows = (rms_scale(projected[:, head_index, 1]) * qk_gains[head_index, 1]).astype(jnp.bfloat16)
        out_grad = (-rate_row[:, None] * projected[:, head_index, 2]).astype(jnp.bfloat16)
        output, updated = head_update(queries, key_rows, out_grad, fasts[head_index], norms[head_index])
        normed_out = (rms_scale(output) * out_gains[head_index]).astype(jnp.bfloat16)
        mixed = mixed + jnp.dot(normed_out, out_weights[head_index], preferred_element_type=jnp.float32)
        new_fasts.append(updated)
    return ((values + mixed).astype(jnp.bfloat16), new_fasts)

def reference(stream, in_gain, w_qkv, qk_gain, w_one, w_three, w_two, token_rate, out_gain, w_out):
    results = []
    for section in range(SECTIONS):
        fasts = []
        norms = []
        for head_index in range(HEADS):
            weights = (w_one[section, head_index].astype(jnp.float32), w_three[section, head_index].astype(jnp.float32), w_two[section, head_index].astype(jnp.float32))
            fasts.append(weights)
            norms.append(tuple((jnp.sqrt(lax.optimization_barrier(jnp.sum(matrix * matrix, axis=0))) for matrix in weights)))
        section_out = []
        for span_index in range(SPANS):
            if section == 0:
                source = stream[span_index]
            else:
                source = results[section - 1][span_index]
            result, fasts = run_section(source, in_gain[section], w_qkv[section], qk_gain[section], token_rate[section, span_index], out_gain[section], w_out[section], fasts, norms)
            section_out.append(result)
        results.append(section_out)
    return jnp.stack([jnp.stack(section_out) for section_out in results])
```

```python
import jax
import jax.numpy as jnp
from jax import lax
from jax.sharding import PartitionSpec as P

NS_STEPS = 2


ns_first = 3.4445
ns_second = -4.775
ns_third = 2.0315
update_step = 1.0
norm_eps = 1e-06
grad_eps = 1e-07


def shifted(array, axis, by):
    devices = lax.axis_size(axis)
    pairs = [(i, i + by) for i in range(devices) if 0 <= i + by < devices]
    return lax.ppermute(array, axis, pairs)


def rms_scale(values):
    return values * lax.rsqrt(jnp.mean(values * values, axis=-1, keepdims=True) + norm_eps)


def contract_rows(left, right):
    return lax.dot_general(
        left, right, (((0,), (0,)), ((), ())), preferred_element_type=jnp.float32
    )


def renormalize(weights, target_norms):
    return weights * (target_norms / (jnp.sqrt(jnp.sum(weights * weights, axis=0)) + norm_eps))


def dot(left, right):
    return jnp.dot(left, right, preferred_element_type=jnp.float32)


def orthogonalize(gradient):
    current = (gradient / (jnp.sqrt(jnp.sum(gradient * gradient)) + grad_eps)).astype(jnp.bfloat16)
    for sweep_index in range(NS_STEPS):
        gram_matrix = lax.dot_general(
            current, current, (((1,), (1,)), ((), ())), preferred_element_type=jnp.float32
        ).astype(jnp.bfloat16)
        square = dot(gram_matrix, gram_matrix)
        mixing = (ns_second * gram_matrix.astype(jnp.float32) + ns_third * square).astype(
            jnp.bfloat16
        )
        current = (ns_first * current.astype(jnp.float32) + dot(mixing, current)).astype(
            jnp.bfloat16
        )
    return current


def gather_heads(block):
    heads = lax.axis_size("head")
    spread = jnp.broadcast_to(block[None], (heads,) + block.shape)
    return lax.all_to_all(spread, "head", split_axis=0, concat_axis=0, tiled=True)


def run_section(
    residual, gain_row, qkv_matrix, head_gains, rate_row, out_gain_row, out_weights, fasts, norms
):
    values = residual.astype(jnp.float32)
    rows, width = residual.shape
    heads = lax.axis_size("head")
    head_width = head_gains.shape[-1]
    whole = gather_heads(residual).swapaxes(0, 1).reshape(rows, heads * width)
    normed = (rms_scale(whole.astype(jnp.float32)) * gain_row).astype(jnp.bfloat16)
    projected = dot(normed, qkv_matrix).reshape(rows, 3, head_width)
    queries = (rms_scale(projected[:, 0]) * head_gains[0]).astype(jnp.bfloat16)
    key_rows = (rms_scale(projected[:, 1]) * head_gains[1]).astype(jnp.bfloat16)
    out_grad = (-rate_row[:, None] * projected[:, 2]).astype(jnp.bfloat16)
    both = lax.all_gather(
        jnp.concatenate([key_rows, out_grad], axis=1), "seq", axis=0, tiled=True
    )
    keys, grads = both[:, :head_width], both[:, head_width:]
    gate_fast, up_fast, down_fast = fasts
    pre_gate = dot(keys, gate_fast.astype(jnp.bfloat16))
    pre_up = dot(keys, up_fast.astype(jnp.bfloat16))
    sigmoid_gate = jax.nn.sigmoid(pre_gate)
    gated = pre_gate * sigmoid_gate
    hidden = (gated * pre_up).astype(jnp.bfloat16)
    backward = lax.dot_general(
        grads,
        down_fast.astype(jnp.bfloat16),
        (((1,), (1,)), ((), ())),
        preferred_element_type=jnp.float32,
    )
    grad_gate = (backward * pre_up * sigmoid_gate * (1.0 + pre_gate * (1.0 - sigmoid_gate))).astype(
        jnp.bfloat16
    )
    grad_up = (backward * gated).astype(jnp.bfloat16)
    gate_step = orthogonalize(contract_rows(keys, grad_gate))
    up_step = orthogonalize(contract_rows(keys, grad_up))
    down_step = orthogonalize(contract_rows(grads, hidden))
    gate_fast = renormalize(gate_fast - update_step * gate_step.astype(jnp.float32), norms[0])
    up_fast = renormalize(up_fast - update_step * up_step.astype(jnp.float32), norms[1])
    down_fast = renormalize(down_fast - update_step * down_step.astype(jnp.float32).T, norms[2])
    gate_out = dot(queries, gate_fast.astype(jnp.bfloat16))
    up_out = dot(queries, up_fast.astype(jnp.bfloat16))
    output = dot(
        (jax.nn.silu(gate_out) * up_out).astype(jnp.bfloat16), down_fast.astype(jnp.bfloat16)
    )
    normed_out = (rms_scale(output) * out_gain_row).astype(jnp.bfloat16)
    head_terms = dot(normed_out, out_weights).astype(jnp.bfloat16)
    terms = head_terms.reshape(rows, heads, width).swapaxes(0, 1)
    parts = lax.all_to_all(terms, "head", split_axis=0, concat_axis=0, tiled=True)
    delta = jnp.sum(parts.astype(jnp.float32), axis=0)
    return ((values + delta).astype(jnp.bfloat16), (gate_fast, up_fast, down_fast))


def shards(stream, in_gain, w_qkv, qk_gain, w_one, w_three, w_two, token_rate, out_gain, w_out):
    segment_index = lax.axis_index("segment")
    span_count = stream.shape[0]
    moments = span_count + lax.axis_size("segment") - 1
    qkv_matrix = w_qkv[0].reshape(w_qkv.shape[1], -1)
    fasts = (
        w_one[0, 0].astype(jnp.float32),
        w_three[0, 0].astype(jnp.float32),
        w_two[0, 0].astype(jnp.float32),
    )
    norms = tuple((jnp.sqrt(jnp.sum(matrix * matrix, axis=0)) for matrix in fasts))
    received = jnp.zeros_like(stream[0])
    collected = jnp.zeros(stream.shape, jnp.bfloat16)
    for moment in range(moments):
        span_index = moment - segment_index
        active = (span_index >= 0) & (span_index < span_count)
        clipped = jnp.clip(span_index, 0, span_count - 1)
        source = jnp.where(segment_index == 0, stream[min(moment, span_count - 1)], received)
        rate_row = lax.dynamic_index_in_dim(token_rate[0], clipped, 0, keepdims=False)
        result, updated = run_section(
            source,
            in_gain[0],
            qkv_matrix,
            qk_gain[0, 0],
            rate_row,
            out_gain[0, 0],
            w_out[0, 0],
            fasts,
            norms,
        )
        fasts = tuple((jnp.where(active, fresh, former) for fresh, former in zip(updated, fasts)))
        chosen = jnp.arange(span_count) == span_index
        collected = jnp.where(chosen[:, None, None], result[None], collected)
        if moment + 1 < moments:
            received = shifted(result, "segment", 1)
    return collected[None]


def solution(mesh):
    placed = (
        P(None, "seq", "head"),
        P("segment", None),
        P("segment", None, "head", None, None),
        P("segment", "head", None, None),
        P("segment", "head", None, None),
        P("segment", "head", None, None),
        P("segment", "head", None, None),
        P("segment", None, "seq"),
        P("segment", "head", None),
        P("segment", "head", None, None),
    )
    return jax.shard_map(
        shards,
        mesh=mesh,
        in_specs=placed,
        out_specs=P("segment", None, "seq", "head"),
        check_vma=False,
    )
```

```python
import jax
import jax.numpy as jnp
from jax import lax
from jax.experimental import pallas as pl
from jax.experimental.pallas import tpu as pltpu
from jax.sharding import PartitionSpec as P

NS_STEPS = 2


ns_first = 3.4445
ns_second = -4.775
ns_third = 2.0315
update_step = 1.0
norm_eps = 1e-06
grad_eps = 1e-07


def shifted(array, axis, by):
    devices = lax.axis_size(axis)
    pairs = [(i, i + by) for i in range(devices) if 0 <= i + by < devices]
    return lax.ppermute(array, axis, pairs)


def rms_scale(values):
    return values * lax.rsqrt(jnp.mean(values * values, axis=-1, keepdims=True) + norm_eps)


def dot(left, right):
    return jnp.dot(left, right, preferred_element_type=jnp.float32)


def contract(left, right, dims):
    return lax.dot_general(
        left, right, ((dims[:1], dims[1:]), ((), ())), preferred_element_type=jnp.float32
    )


def fast_kernel(
    active_ref,
    both_ref,
    query_ref,
    gate_ref,
    up_ref,
    down_ref,
    wide_norms_ref,
    down_norm_ref,
    out_gain_ref,
    out_weights_hbm,
    terms_ref,
    new_gate_ref,
    new_up_ref,
    new_down_ref,
    rights,
    work,
    out_weights,
    out_sem,
):
    fetch = pltpu.make_async_copy(out_weights_hbm, out_weights, out_sem)
    fetch.start()
    tokens = both_ref.shape[1]
    rows = query_ref.shape[0]
    chunk = 2 * rows if tokens % (2 * rows) == 0 else rows
    work[0] = gate_ref[...].astype(jnp.bfloat16)
    work[1] = up_ref[...].astype(jnp.bfloat16)
    work[2] = down_ref[...].astype(jnp.bfloat16)

    def gradients(index, carry):
        here = pl.ds(pl.multiple_of(index * chunk, chunk), chunk)
        keys = both_ref[0, here, :]
        grads = both_ref[1, here, :]
        pre_gate = dot(keys, work[0])
        pre_up = dot(keys, work[1])
        backward = dot(grads, work[2])
        sigmoid_gate = jax.nn.sigmoid(pre_gate)
        gated = pre_gate * sigmoid_gate
        rights[0, here, :] = (
            backward * pre_up * sigmoid_gate * (1.0 + pre_gate * (1.0 - sigmoid_gate))
        ).astype(jnp.bfloat16)
        rights[1, here, :] = (backward * gated).astype(jnp.bfloat16)
        rights[2, here, :] = (gated * pre_up).astype(jnp.bfloat16)
        return carry

    lax.fori_loop(0, tokens // chunk, gradients, 0)

    def orthogonalize(index, carry):
        gradient = contract(both_ref[index // 2], rights[index], (0, 0))
        scale = 1.0 / (jnp.sqrt(jnp.sum(gradient * gradient, keepdims=True)) + grad_eps)
        work[index] = (gradient * scale).astype(jnp.bfloat16)

        def sweep(step, inner):
            current = work[index]
            gram_matrix = contract(current, current, (1, 1)).astype(jnp.bfloat16)
            square = dot(gram_matrix, gram_matrix)
            mixing = (ns_second * gram_matrix.astype(jnp.float32) + ns_third * square).astype(
                jnp.bfloat16
            )
            work[index] = (ns_first * current.astype(jnp.float32) + dot(mixing, current)).astype(
                jnp.bfloat16
            )
            return inner

        return lax.fori_loop(0, NS_STEPS, sweep, carry)

    lax.fori_loop(0, 3, orthogonalize, 0)

    active = active_ref[0] > 0
    for index, old_ref, new_ref, axis, target in (
        (0, gate_ref, new_gate_ref, 0, wide_norms_ref[0]),
        (1, up_ref, new_up_ref, 0, wide_norms_ref[1]),
        (2, down_ref, new_down_ref, 1, down_norm_ref[...]),
    ):
        moved = old_ref[...] - update_step * work[index].astype(jnp.float32)
        length = jnp.sqrt(jnp.sum(moved * moved, axis=axis, keepdims=True)) + norm_eps
        fresh = moved * (target / length)
        work[index] = fresh.astype(jnp.bfloat16)
        new_ref[...] = jnp.where(active, fresh, old_ref[...])

    gate_out = dot(query_ref[...], work[0])
    up_out = dot(query_ref[...], work[1])
    inner = (gate_out * jax.nn.sigmoid(gate_out) * up_out).astype(jnp.bfloat16)
    output = contract(inner, work[2], (1, 1))
    normed_out = (rms_scale(output) * out_gain_ref[...]).astype(jnp.bfloat16)
    fetch.wait()
    width = terms_ref.shape[2]

    def project(index, carry):
        columns = pl.ds(pl.multiple_of(index * width, width), width)
        terms_ref[index] = dot(normed_out, out_weights[:, columns]).astype(jnp.bfloat16)
        return carry

    lax.fori_loop(0, terms_ref.shape[0], project, 0)


def fast_step(active, both, queries, fasts, norms, out_gain_row, out_weights, heads):
    rows = queries.shape[0]
    inner, wide = fasts[0].shape
    width = out_weights.shape[1] // heads
    vmem = pl.BlockSpec(memory_space=pltpu.VMEM)
    state = jax.ShapeDtypeStruct((inner, wide), jnp.float32)
    return pl.pallas_call(
        fast_kernel,
        name="fast_step",
        out_shape=(jax.ShapeDtypeStruct((heads, rows, width), jnp.bfloat16), state, state, state),
        in_specs=[pl.BlockSpec(memory_space=pltpu.SMEM)]
        + [vmem] * 8
        + [pl.BlockSpec(memory_space=pl.ANY)],
        out_specs=(vmem,) * 4,
        scratch_shapes=[
            pltpu.VMEM((3, both.shape[1], wide), jnp.bfloat16),
            pltpu.VMEM((3, inner, wide), jnp.bfloat16),
            pltpu.VMEM(out_weights.shape, jnp.bfloat16),
            pltpu.SemaphoreType.DMA,
        ],
        compiler_params=pltpu.CompilerParams(vmem_limit_bytes=60 * 1024 * 1024),
        cost_estimate=pl.CostEstimate(
            flops=10**10, bytes_accessed=2 * 10**7, transcendentals=0
        ),
    )(active, both, queries, *fasts, *norms, out_gain_row, out_weights)


def gather_heads(block):
    heads = lax.axis_size("head")
    spread = jnp.broadcast_to(block[None], (heads,) + block.shape)
    return lax.all_to_all(spread, "head", split_axis=0, concat_axis=0, tiled=True)


def run_section(
    residual, gain_row, qkv_matrix, head_gains, rate_row, out_gain_row, out_weights, fasts, norms, active
):
    values = residual.astype(jnp.float32)
    rows, width = residual.shape
    heads = lax.axis_size("head")
    head_width = head_gains.shape[-1]
    whole = gather_heads(residual).swapaxes(0, 1).reshape(rows, heads * width)
    normed = (rms_scale(whole.astype(jnp.float32)) * gain_row).astype(jnp.bfloat16)
    projected = dot(normed, qkv_matrix).reshape(rows, 3, head_width)
    queries = (rms_scale(projected[:, 0]) * head_gains[0]).astype(jnp.bfloat16)
    key_rows = (rms_scale(projected[:, 1]) * head_gains[1]).astype(jnp.bfloat16)
    out_grad = (-rate_row[:, None] * projected[:, 2]).astype(jnp.bfloat16)
    both = lax.all_gather(jnp.stack([key_rows, out_grad]), "seq", axis=1, tiled=True)
    terms, *fasts = fast_step(
        active, both, queries, fasts, norms, out_gain_row, out_weights, heads
    )
    parts = lax.all_to_all(terms, "head", split_axis=0, concat_axis=0, tiled=True)
    delta = jnp.sum(parts.astype(jnp.float32), axis=0)
    return ((values + delta).astype(jnp.bfloat16), tuple(fasts))


def shards(stream, in_gain, w_qkv, qk_gain, w_one, w_three, w_two, token_rate, out_gain, w_out):
    segment_index = lax.axis_index("segment")
    span_count = stream.shape[0]
    moments = span_count + lax.axis_size("segment") - 1
    qkv_matrix = w_qkv[0].reshape(w_qkv.shape[1], -1)
    fasts = (
        w_one[0, 0].astype(jnp.float32),
        w_three[0, 0].astype(jnp.float32),
        w_two[0, 0].astype(jnp.float32).T,
    )
    norms = (
        jnp.stack([jnp.sqrt(jnp.sum(matrix * matrix, axis=0, keepdims=True)) for matrix in fasts[:2]]),
        jnp.sqrt(jnp.sum(fasts[2] * fasts[2], axis=1, keepdims=True)),
    )
    received = jnp.zeros_like(stream[0])
    collected = jnp.zeros(stream.shape, jnp.bfloat16)
    for moment in range(moments):
        span_index = moment - segment_index
        active = (span_index >= 0) & (span_index < span_count)
        clipped = jnp.clip(span_index, 0, span_count - 1)
        source = jnp.where(segment_index == 0, stream[min(moment, span_count - 1)], received)
        rate_row = lax.dynamic_index_in_dim(token_rate[0], clipped, 0, keepdims=False)
        result, fasts = run_section(
            source,
            in_gain[0],
            qkv_matrix,
            qk_gain[0, 0],
            rate_row,
            out_gain[0, :1],
            w_out[0, 0],
            fasts,
            norms,
            active.astype(jnp.int32)[None],
        )
        chosen = jnp.arange(span_count) == span_index
        collected = jnp.where(chosen[:, None, None], result[None], collected)
        if moment + 1 < moments:
            received = shifted(result, "segment", 1)
    return collected[None]


def solution(mesh):
    placed = (
        P(None, "seq", "head"),
        P("segment", None),
        P("segment", None, "head", None, None),
        P("segment", "head", None, None),
        P("segment", "head", None, None),
        P("segment", "head", None, None),
        P("segment", "head", None, None),
        P("segment", None, "seq"),
        P("segment", "head", None),
        P("segment", "head", None, None),
    )
    return jax.shard_map(
        shards,
        mesh=mesh,
        in_specs=placed,
        out_specs=P("segment", None, "seq", "head"),
        check_vma=False,
    )
```

```python
import functools

import jax
import jax.numpy as jnp
from jax import lax
from jax.experimental import pallas as pl
from jax.experimental.pallas import tpu as pltpu
from jax.sharding import PartitionSpec as P

NS_STEPS = 2


ns_first = 3.4445
ns_second = -4.775
ns_third = 2.0315
update_step = 1.0
norm_eps = 1e-06
grad_eps = 1e-07


def rms_scale(values):
    return values * lax.rsqrt(jnp.mean(values * values, axis=-1, keepdims=True) + norm_eps)


def dot(left, right):
    return jnp.dot(left, right, preferred_element_type=jnp.float32)


def contract(left, right, dims):
    return lax.dot_general(
        left, right, ((dims[:1], dims[1:]), ((), ())), preferred_element_type=jnp.float32
    )


def fast_kernel(
    active_ref,
    both_ref,
    query_ref,
    gate_ref,
    up_ref,
    down_ref,
    wide_norms_ref,
    down_norm_ref,
    out_gain_ref,
    out_weights_hbm,
    terms_ref,
    new_gate_ref,
    new_up_ref,
    new_down_ref,
    rights,
    work,
    out_weights,
    out_sem,
):
    fetch = pltpu.make_async_copy(out_weights_hbm, out_weights, out_sem)
    fetch.start()
    tokens = both_ref.shape[1]
    rows = query_ref.shape[0]
    chunk = 2 * rows if tokens % (2 * rows) == 0 else rows
    work[0] = gate_ref[...].astype(jnp.bfloat16)
    work[1] = up_ref[...].astype(jnp.bfloat16)
    work[2] = down_ref[...].astype(jnp.bfloat16)

    def gradients(index, carry):
        here = pl.ds(pl.multiple_of(index * chunk, chunk), chunk)
        keys = both_ref[0, here, :]
        grads = both_ref[1, here, :]
        pre_gate = dot(keys, work[0])
        pre_up = dot(keys, work[1])
        backward = dot(grads, work[2])
        sigmoid_gate = jax.nn.sigmoid(pre_gate)
        gated = pre_gate * sigmoid_gate
        rights[0, here, :] = (
            backward * pre_up * sigmoid_gate * (1.0 + pre_gate * (1.0 - sigmoid_gate))
        ).astype(jnp.bfloat16)
        rights[1, here, :] = (backward * gated).astype(jnp.bfloat16)
        rights[2, here, :] = (gated * pre_up).astype(jnp.bfloat16)
        return carry

    lax.fori_loop(0, tokens // chunk, gradients, 0)

    def orthogonalize(index, carry):
        gradient = contract(both_ref[index // 2], rights[index], (0, 0))
        scale = 1.0 / (jnp.sqrt(jnp.sum(gradient * gradient, keepdims=True)) + grad_eps)
        work[index] = (gradient * scale).astype(jnp.bfloat16)

        def sweep(step, inner):
            current = work[index]
            gram_matrix = contract(current, current, (1, 1)).astype(jnp.bfloat16)
            square = dot(gram_matrix, gram_matrix)
            mixing = (ns_second * gram_matrix.astype(jnp.float32) + ns_third * square).astype(
                jnp.bfloat16
            )
            work[index] = (ns_first * current.astype(jnp.float32) + dot(mixing, current)).astype(
                jnp.bfloat16
            )
            return inner

        return lax.fori_loop(0, NS_STEPS, sweep, carry)

    lax.fori_loop(0, 3, orthogonalize, 0)

    active = active_ref[0] > 0
    for index, old_ref, new_ref, axis, target in (
        (0, gate_ref, new_gate_ref, 0, wide_norms_ref[0]),
        (1, up_ref, new_up_ref, 0, wide_norms_ref[1]),
        (2, down_ref, new_down_ref, 1, down_norm_ref[...]),
    ):
        moved = old_ref[...] - update_step * work[index].astype(jnp.float32)
        length = jnp.sqrt(jnp.sum(moved * moved, axis=axis, keepdims=True)) + norm_eps
        fresh = moved * (target / length)
        work[index] = fresh.astype(jnp.bfloat16)
        new_ref[...] = jnp.where(active, fresh, old_ref[...])

    gate_out = dot(query_ref[...], work[0])
    up_out = dot(query_ref[...], work[1])
    inner = (gate_out * jax.nn.sigmoid(gate_out) * up_out).astype(jnp.bfloat16)
    output = contract(inner, work[2], (1, 1))
    normed_out = (rms_scale(output) * out_gain_ref[...]).astype(jnp.bfloat16)
    fetch.wait()
    width = terms_ref.shape[2]

    def project(index, carry):
        columns = pl.ds(pl.multiple_of(index * width, width), width)
        terms_ref[index] = dot(normed_out, out_weights[:, columns]).astype(jnp.bfloat16)
        return carry

    lax.fori_loop(0, terms_ref.shape[0], project, 0)


def fast_step(active, both, queries, fasts, norms, out_gain_row, out_weights, heads):
    rows = queries.shape[0]
    inner, wide = fasts[0].shape
    width = out_weights.shape[1] // heads
    vmem = pl.BlockSpec(memory_space=pltpu.VMEM)
    state = jax.ShapeDtypeStruct((inner, wide), jnp.float32)
    return pl.pallas_call(
        fast_kernel,
        name="fast_step",
        out_shape=(jax.ShapeDtypeStruct((heads, rows, width), jnp.bfloat16), state, state, state),
        in_specs=[pl.BlockSpec(memory_space=pltpu.SMEM)]
        + [vmem] * 8
        + [pl.BlockSpec(memory_space=pl.ANY)],
        out_specs=(vmem,) * 4,
        scratch_shapes=[
            pltpu.VMEM((3, both.shape[1], wide), jnp.bfloat16),
            pltpu.VMEM((3, inner, wide), jnp.bfloat16),
            pltpu.VMEM(out_weights.shape, jnp.bfloat16),
            pltpu.SemaphoreType.DMA,
        ],
        compiler_params=pltpu.CompilerParams(vmem_limit_bytes=60 * 1024 * 1024),
        cost_estimate=pl.CostEstimate(
            flops=10**10, bytes_accessed=2 * 10**7, transcendentals=0
        ),
    )(active, both, queries, *fasts, *norms, out_gain_row, out_weights)


def signal(semaphore, target):
    pl.semaphore_signal(
        semaphore, inc=1, device_id=target, device_id_type=pl.DeviceIdType.MESH
    )


def remote(source, target, send_sem, recv_sem, device):
    return pltpu.make_async_remote_copy(
        src_ref=source,
        dst_ref=target,
        send_sem=send_sem,
        recv_sem=recv_sem,
        device_id=device,
        device_id_type=pl.DeviceIdType.MESH,
    )


def gather_tokens_kernel(devices, own_ref, all_ref, send_sems, recv_sems, pair_sends, pair_recvs, own_sem):
    me = lax.axis_index("seq")
    chips = devices // 2
    chip, core = me // 2, lax.rem(me, 2)
    partner = {"seq": 2 * chip + 1 - core}
    parts, rows = own_ref.shape[0], own_ref.shape[1]
    barrier = pltpu.get_barrier_semaphore()
    signal(barrier, partner)
    for step in range(1, chips):
        signal(barrier, {"seq": 2 * lax.rem(chip + step, chips) + core})
    pl.semaphore_wait(barrier, chips)

    def place(part, origin):
        return all_ref.at[part, pl.ds(pl.multiple_of(origin * rows, rows), rows), :]

    far, near = {}, {}
    for part in range(parts):
        for step in range(1, chips):
            far[part, step] = remote(
                own_ref.at[part],
                place(part, me),
                send_sems.at[part, step],
                recv_sems.at[part, step],
                {"seq": 2 * lax.rem(chip + step, chips) + core},
            )
            far[part, step].start()
        near[part, 0] = remote(
            own_ref.at[part], place(part, me), pair_sends.at[part, 0], pair_recvs.at[part, 0], partner
        )
        near[part, 0].start()
    copies = []
    for part in range(parts):
        copies.append(pltpu.make_async_copy(own_ref.at[part], place(part, me), own_sem.at[part]))
        copies[-1].start()
    for part in range(parts):
        for step in range(1, chips):
            far[part, step].wait_recv()
            origin = 2 * lax.rem(chip + chips - step, chips) + core
            near[part, step] = remote(
                place(part, origin),
                place(part, origin),
                pair_sends.at[part, step],
                pair_recvs.at[part, step],
                partner,
            )
            near[part, step].start()
    for copy in copies:
        copy.wait()
    for copy in far.values():
        copy.wait_send()
    for copy in near.values():
        copy.wait_send()
        copy.wait_recv()


def gather_tokens(own):
    devices = lax.axis_size("seq")
    parts, rows, width = own.shape
    vmem = pl.BlockSpec(memory_space=pltpu.VMEM)
    return pl.pallas_call(
        functools.partial(gather_tokens_kernel, devices),
        name="gather_tokens",
        out_shape=jax.ShapeDtypeStruct((parts, devices * rows, width), own.dtype),
        in_specs=[vmem],
        out_specs=vmem,
        scratch_shapes=[pltpu.SemaphoreType.DMA((parts, devices // 2))] * 4
        + [pltpu.SemaphoreType.DMA((parts,))],
        compiler_params=pltpu.CompilerParams(
            collective_id=0, has_side_effects=True, vmem_limit_bytes=16 * 1024 * 1024
        ),
    )(own)


def exchange_kernel(heads, segments, chunks, onward, *refs):
    if onward:
        terms_ref, residual_ref, stream_ref, result_ref, whole_ref = refs[:5]
        slots, total, sum_sends, sum_recvs, copy_sends, copy_recvs, hop_sends, hop_recvs, own_sem = refs[5:]
    else:
        terms_ref, residual_ref, result_ref, slots, total, sum_sends, sum_recvs = refs
    me = lax.axis_index("head")
    segment = lax.axis_index("segment")
    rows, width = residual_ref.shape
    piece = rows // chunks
    has_left, has_right = me >= 1, me + 1 < heads
    barrier = pltpu.get_barrier_semaphore()
    awaited = has_left.astype(jnp.int32) + has_right.astype(jnp.int32)

    @pl.when(has_left)
    def _():
        signal(barrier, {"head": me - 1})

    @pl.when(has_right)
    def _():
        signal(barrier, {"head": me + 1})

    if onward:
        awaited = awaited + (segment + 1 < segments).astype(jnp.int32)

        @pl.when(segment >= 1)
        def _():
            signal(barrier, {"segment": segment - 1})

    pl.semaphore_wait(barrier, awaited)

    def rows_of(chunk):
        return pl.ds(chunk * piece, piece)

    def within(position):
        return (position >= 0) & (position < heads)

    sides = ((0, 1), (1, -1))

    def sum_copy(side, sign, distance, chunk, first):
        source = (
            terms_ref.at[me + sign * distance, rows_of(chunk), :]
            if first
            else slots.at[side, distance, rows_of(chunk), :]
        )
        return remote(
            source,
            slots.at[side, distance - 1, rows_of(chunk), :],
            sum_sends.at[side, distance, chunk],
            sum_recvs.at[side, distance - 1, chunk],
            {"head": me + sign},
        )

    def sum_arrival(side, sign, distance, chunk):
        return remote(
            slots.at[side, distance, rows_of(chunk), :],
            slots.at[side, distance, rows_of(chunk), :],
            sum_sends.at[side, distance, chunk],
            sum_recvs.at[side, distance, chunk],
            {"head": me - sign},
        )

    def send_sums(distance, chunk):
        for side, sign in sides:

            @pl.when(within(me + sign * distance) & jnp.logical_not(within(me - sign)))
            def _():
                sum_copy(side, sign, distance, chunk, True).start()

            if distance < heads - 1:

                @pl.when(within(me + sign * distance) & within(me - sign))
                def _():
                    sum_arrival(side, sign, distance, chunk).wait_recv()
                    here = rows_of(chunk)
                    slots[side, distance, here, :] = (
                        slots[side, distance, here, :].astype(jnp.float32)
                        + terms_ref[me + sign * distance, here, :].astype(jnp.float32)
                    ).astype(jnp.bfloat16)
                    sum_copy(side, sign, distance, chunk, False).start()

    def finish(chunk):
        here = rows_of(chunk)
        total[...] = residual_ref[here, :].astype(jnp.float32) + terms_ref[me, here, :].astype(
            jnp.float32
        )
        for side, sign in sides:

            @pl.when(within(me - sign))
            def _():
                sum_arrival(side, sign, 0, chunk).wait_recv()
                total[...] += slots[side, 0, here, :].astype(jnp.float32)

        result_ref[here, :] = total[...].astype(jnp.bfloat16)
        if onward:

            @pl.when(segment + 1 < segments)
            def _():
                hop(chunk).start()

    def place(origin, chunk):
        return whole_ref.at[
            rows_of(chunk), pl.ds(pl.multiple_of(origin * width, width), width)
        ]

    def hop(chunk):
        return remote(
            result_ref.at[rows_of(chunk), :],
            place(me, chunk),
            hop_sends.at[chunk],
            hop_recvs.at[chunk],
            {"segment": segment + 1},
        )

    def hop_arrival(chunk):
        return remote(
            place(me, chunk),
            place(me, chunk),
            hop_sends.at[chunk],
            hop_recvs.at[chunk],
            {"segment": segment - 1},
        )

    def block_copy(side, sign, step, chunk):
        origin = me - sign * step
        return remote(
            place(origin, chunk),
            place(origin, chunk),
            copy_sends.at[side, step, chunk],
            copy_recvs.at[side, step, chunk],
            {"head": me + sign},
        )

    def block_arrival(side, sign, step, chunk):
        origin = me - sign * (step + 1)
        return remote(
            place(origin, chunk),
            place(origin, chunk),
            copy_sends.at[side, step, chunk],
            copy_recvs.at[side, step, chunk],
            {"head": me - sign},
        )

    def send_blocks(step, chunk):
        if step == 0:

            @pl.when(segment >= 1)
            def _():
                hop_arrival(chunk).wait_recv()

        for side, sign in sides:
            if step > 0:

                @pl.when(within(me - sign * step))
                def _():
                    block_arrival(side, sign, step - 1, chunk).wait_recv()

            if step < heads - 1:

                @pl.when(within(me - sign * step) & within(me + sign))
                def _():
                    block_copy(side, sign, step, chunk).start()

    if onward:
        own = pltpu.make_async_copy(
            stream_ref, whole_ref.at[:, pl.ds(pl.multiple_of(me * width, width), width)], own_sem
        )

        @pl.when(segment == 0)
        def _():
            own.start()
            own.wait()

    stages = [functools.partial(send_sums, distance) for distance in range(heads - 1, 0, -1)]
    stages.append(finish)
    if onward:
        stages += [functools.partial(send_blocks, step) for step in range(heads)]
    for moment in range(chunks + len(stages) - 1):
        for index, stage in enumerate(stages):
            if 0 <= moment - index < chunks:
                stage(moment - index)

    for chunk in range(chunks):
        for side, sign in sides:
            for distance in range(1, heads):

                @pl.when(within(me + sign * distance))
                def _():
                    sum_copy(side, sign, distance, chunk, True).wait_send()

            if onward:
                for step in range(heads - 1):

                    @pl.when(within(me - sign * step) & within(me + sign))
                    def _():
                        block_copy(side, sign, step, chunk).wait_send()

        if onward:

            @pl.when(segment + 1 < segments)
            def _():
                hop(chunk).wait_send()


def exchange(terms, residual, following):
    heads, rows, width = terms.shape
    segments = lax.axis_size("segment")
    onward = following is not None
    chunks = 4
    vmem = pl.BlockSpec(memory_space=pltpu.VMEM)
    shapes = [jax.ShapeDtypeStruct((rows, width), jnp.bfloat16)]
    scratch = [
        pltpu.VMEM((2, heads, rows, width), jnp.bfloat16),
        pltpu.VMEM((rows // chunks, width), jnp.float32),
    ] + [pltpu.SemaphoreType.DMA((2, heads, chunks))] * 2
    operands = [terms, residual]
    if onward:
        operands.append(following)
        shapes.append(jax.ShapeDtypeStruct((rows, heads * width), jnp.bfloat16))
        scratch += [pltpu.SemaphoreType.DMA((2, heads, chunks))] * 2
        scratch += [pltpu.SemaphoreType.DMA((chunks,))] * 2 + [pltpu.SemaphoreType.DMA]
    return pl.pallas_call(
        functools.partial(exchange_kernel, heads, segments, chunks, onward),
        name="exchange" if onward else "reduce",
        out_shape=tuple(shapes),
        in_specs=[vmem] * len(operands),
        out_specs=(vmem,) * len(shapes),
        scratch_shapes=scratch,
        compiler_params=pltpu.CompilerParams(
            collective_id=1 if onward else 2,
            has_side_effects=True,
            vmem_limit_bytes=24 * 1024 * 1024,
        ),
    )(*operands)


def gather_heads(block):
    heads = lax.axis_size("head")
    spread = jnp.broadcast_to(block[None], (heads,) + block.shape)
    return lax.all_to_all(spread, "head", split_axis=0, concat_axis=0, tiled=True)


def run_section(
    whole, gain_row, qkv_matrix, head_gains, rate_row, out_gain_row, out_weights, fasts, norms, active
):
    rows = whole.shape[0]
    heads = lax.axis_size("head")
    head_width = head_gains.shape[-1]
    normed = (rms_scale(whole.astype(jnp.float32)) * gain_row).astype(jnp.bfloat16)
    projected = dot(normed, qkv_matrix).reshape(rows, 3, head_width)
    queries = (rms_scale(projected[:, 0]) * head_gains[0]).astype(jnp.bfloat16)
    key_rows = (rms_scale(projected[:, 1]) * head_gains[1]).astype(jnp.bfloat16)
    out_grad = (-rate_row[:, None] * projected[:, 2]).astype(jnp.bfloat16)
    both = gather_tokens(jnp.stack([key_rows, out_grad]))
    return fast_step(active, both, queries, fasts, norms, out_gain_row, out_weights, heads)


def shards(stream, in_gain, w_qkv, qk_gain, w_one, w_three, w_two, token_rate, out_gain, w_out):
    segment_index = lax.axis_index("segment")
    span_count = stream.shape[0]
    moments = span_count + lax.axis_size("segment") - 1
    qkv_matrix = w_qkv[0].reshape(w_qkv.shape[1], -1)
    fasts = (
        w_one[0, 0].astype(jnp.float32),
        w_three[0, 0].astype(jnp.float32),
        w_two[0, 0].astype(jnp.float32).T,
    )
    norms = (
        jnp.stack([jnp.sqrt(jnp.sum(matrix * matrix, axis=0, keepdims=True)) for matrix in fasts[:2]]),
        jnp.sqrt(jnp.sum(fasts[2] * fasts[2], axis=1, keepdims=True)),
    )
    collected = jnp.zeros(stream.shape, jnp.bfloat16)
    source = stream[0]
    whole = gather_heads(source).swapaxes(0, 1).reshape(source.shape[0], -1)
    for moment in range(moments):
        span_index = moment - segment_index
        active = (span_index >= 0) & (span_index < span_count)
        clipped = jnp.clip(span_index, 0, span_count - 1)
        rate_row = lax.dynamic_index_in_dim(token_rate[0], clipped, 0, keepdims=False)
        terms, *fasts = run_section(
            whole,
            in_gain[0],
            qkv_matrix,
            qk_gain[0, 0],
            rate_row,
            out_gain[0, :1],
            w_out[0, 0],
            fasts,
            norms,
            active.astype(jnp.int32)[None],
        )
        if moment + 1 < moments:
            following = stream[min(moment + 1, span_count - 1)]
            result, whole = exchange(terms, source, following)
            source = lax.dynamic_slice_in_dim(
                whole, lax.axis_index("head") * source.shape[1], source.shape[1], axis=1
            )
        else:
            (result,) = exchange(terms, source, None)
        chosen = jnp.arange(span_count) == span_index
        collected = jnp.where(chosen[:, None, None], result[None], collected)
    return collected[None]


def solution(mesh):
    placed = (
        P(None, "seq", "head"),
        P("segment", None),
        P("segment", None, "head", None, None),
        P("segment", "head", None, None),
        P("segment", "head", None, None),
        P("segment", "head", None, None),
        P("segment", "head", None, None),
        P("segment", None, "seq"),
        P("segment", "head", None),
        P("segment", "head", None, None),
    )
    return jax.shard_map(
        shards,
        mesh=mesh,
        in_specs=placed,
        out_specs=P("segment", None, "seq", "head"),
        check_vma=False,
    )
```

```python
import functools

import jax
import jax.numpy as jnp
from jax import lax
from jax.experimental import pallas as pl
from jax.experimental.pallas import tpu as pltpu
from jax.sharding import PartitionSpec as P

NS_STEPS = 2


ns_first = 3.4445
ns_second = -4.775
ns_third = 2.0315
update_step = 1.0
norm_eps = 1e-06
grad_eps = 1e-07


def rms_scale(values):
    return values * lax.rsqrt(jnp.mean(values * values, axis=-1, keepdims=True) + norm_eps)


def dot(left, right):
    return jnp.dot(left, right, preferred_element_type=jnp.float32)


def contract(left, right, dims):
    return lax.dot_general(
        left, right, ((dims[:1], dims[1:]), ((), ())), preferred_element_type=jnp.float32
    )


def fast_kernel(
    active_ref,
    both_ref,
    query_ref,
    gate_ref,
    up_ref,
    down_ref,
    wide_norms_ref,
    down_norm_ref,
    out_gain_ref,
    out_weights_hbm,
    terms_ref,
    new_gate_ref,
    new_up_ref,
    new_down_ref,
    rights,
    work,
    out_weights,
    out_sem,
):
    fetch = pltpu.make_async_copy(out_weights_hbm, out_weights, out_sem)
    fetch.start()
    tokens = both_ref.shape[1]
    rows = query_ref.shape[0]
    chunk = 2 * rows if tokens % (2 * rows) == 0 else rows
    work[0] = gate_ref[...].astype(jnp.bfloat16)
    work[1] = up_ref[...].astype(jnp.bfloat16)
    work[2] = down_ref[...].astype(jnp.bfloat16)

    def gradients(index, carry):
        here = pl.ds(pl.multiple_of(index * chunk, chunk), chunk)
        keys = both_ref[0, here, :]
        grads = both_ref[1, here, :]
        pre_gate = dot(keys, work[0])
        pre_up = dot(keys, work[1])
        backward = dot(grads, work[2])
        sigmoid_gate = jax.nn.sigmoid(pre_gate)
        gated = pre_gate * sigmoid_gate
        rights[0, here, :] = (
            backward * pre_up * sigmoid_gate * (1.0 + pre_gate * (1.0 - sigmoid_gate))
        ).astype(jnp.bfloat16)
        rights[1, here, :] = (backward * gated).astype(jnp.bfloat16)
        rights[2, here, :] = (gated * pre_up).astype(jnp.bfloat16)
        return carry

    lax.fori_loop(0, tokens // chunk, gradients, 0)

    def orthogonalize(index, carry):
        gradient = contract(both_ref[index // 2], rights[index], (0, 0))
        scale = 1.0 / (jnp.sqrt(jnp.sum(gradient * gradient, keepdims=True)) + grad_eps)
        work[index] = (gradient * scale).astype(jnp.bfloat16)

        def sweep(step, inner):
            current = work[index]
            gram_matrix = contract(current, current, (1, 1)).astype(jnp.bfloat16)
            square = dot(gram_matrix, gram_matrix)
            mixing = (ns_second * gram_matrix.astype(jnp.float32) + ns_third * square).astype(
                jnp.bfloat16
            )
            work[index] = (ns_first * current.astype(jnp.float32) + dot(mixing, current)).astype(
                jnp.bfloat16
            )
            return inner

        return lax.fori_loop(0, NS_STEPS, sweep, carry)

    lax.fori_loop(0, 3, orthogonalize, 0)

    active = active_ref[0] > 0
    for index, old_ref, new_ref, axis, target in (
        (0, gate_ref, new_gate_ref, 0, wide_norms_ref[0]),
        (1, up_ref, new_up_ref, 0, wide_norms_ref[1]),
        (2, down_ref, new_down_ref, 1, down_norm_ref[...]),
    ):
        moved = old_ref[...] - update_step * work[index].astype(jnp.float32)
        length = jnp.sqrt(jnp.sum(moved * moved, axis=axis, keepdims=True)) + norm_eps
        fresh = moved * (target / length)
        work[index] = fresh.astype(jnp.bfloat16)
        new_ref[...] = jnp.where(active, fresh, old_ref[...])

    gate_out = dot(query_ref[...], work[0])
    up_out = dot(query_ref[...], work[1])
    inner = (gate_out * jax.nn.sigmoid(gate_out) * up_out).astype(jnp.bfloat16)
    output = contract(inner, work[2], (1, 1))
    normed_out = (rms_scale(output) * out_gain_ref[...]).astype(jnp.bfloat16)
    fetch.wait()
    width = terms_ref.shape[2]

    def project(index, carry):
        columns = pl.ds(pl.multiple_of(index * width, width), width)
        terms_ref[index] = dot(normed_out, out_weights[:, columns]).astype(jnp.bfloat16)
        return carry

    lax.fori_loop(0, terms_ref.shape[0], project, 0)


def fast_step(active, both, queries, fasts, norms, out_gain_row, out_weights, heads):
    rows = queries.shape[0]
    inner, wide = fasts[0].shape
    width = out_weights.shape[1] // heads
    vmem = pl.BlockSpec(memory_space=pltpu.VMEM)
    state = jax.ShapeDtypeStruct((inner, wide), jnp.float32)
    held = 4 * both.size + 6 * both.shape[1] * wide + 30 * inner * wide + 2 * out_weights.size
    return pl.pallas_call(
        fast_kernel,
        name="fast_step",
        out_shape=(jax.ShapeDtypeStruct((heads, rows, width), jnp.bfloat16), state, state, state),
        in_specs=[pl.BlockSpec(memory_space=pltpu.SMEM)]
        + [vmem] * 8
        + [pl.BlockSpec(memory_space=pl.ANY)],
        out_specs=(vmem,) * 4,
        scratch_shapes=[
            pltpu.VMEM((3, both.shape[1], wide), jnp.bfloat16),
            pltpu.VMEM((3, inner, wide), jnp.bfloat16),
            pltpu.VMEM(out_weights.shape, jnp.bfloat16),
            pltpu.SemaphoreType.DMA,
        ],
        compiler_params=pltpu.CompilerParams(vmem_limit_bytes=held + 14 * 1024 * 1024),
        cost_estimate=pl.CostEstimate(
            flops=10**10, bytes_accessed=2 * 10**7, transcendentals=0
        ),
    )(active, both, queries, *fasts, *norms, out_gain_row, out_weights)


def signal(semaphore, target):
    pl.semaphore_signal(
        semaphore, inc=1, device_id=target, device_id_type=pl.DeviceIdType.MESH
    )


def remote(source, target, send_sem, recv_sem, device):
    return pltpu.make_async_remote_copy(
        src_ref=source,
        dst_ref=target,
        send_sem=send_sem,
        recv_sem=recv_sem,
        device_id=device,
        device_id_type=pl.DeviceIdType.MESH,
    )


def gather_tokens_kernel(devices, own_ref, all_ref, send_sems, recv_sems, pair_sends, pair_recvs, own_sem):
    me = lax.axis_index("seq")
    chips = devices // 2
    chip, core = me // 2, lax.rem(me, 2)
    partner = {"seq": 2 * chip + 1 - core}
    parts, rows = own_ref.shape[0], own_ref.shape[1]
    barrier = pltpu.get_barrier_semaphore()
    signal(barrier, partner)
    for step in range(1, chips):
        signal(barrier, {"seq": 2 * lax.rem(chip + step, chips) + core})
    pl.semaphore_wait(barrier, chips)

    def place(part, origin):
        return all_ref.at[part, pl.ds(pl.multiple_of(origin * rows, rows), rows), :]

    far, near = {}, {}
    for part in range(parts):
        for step in range(1, chips):
            far[part, step] = remote(
                own_ref.at[part],
                place(part, me),
                send_sems.at[part, step],
                recv_sems.at[part, step],
                {"seq": 2 * lax.rem(chip + step, chips) + core},
            )
            far[part, step].start()
        near[part, 0] = remote(
            own_ref.at[part], place(part, me), pair_sends.at[part, 0], pair_recvs.at[part, 0], partner
        )
        near[part, 0].start()
    copies = []
    for part in range(parts):
        copies.append(pltpu.make_async_copy(own_ref.at[part], place(part, me), own_sem.at[part]))
        copies[-1].start()
    for part in range(parts):
        for step in range(1, chips):
            far[part, step].wait_recv()
            origin = 2 * lax.rem(chip + chips - step, chips) + core
            near[part, step] = remote(
                place(part, origin),
                place(part, origin),
                pair_sends.at[part, step],
                pair_recvs.at[part, step],
                partner,
            )
            near[part, step].start()
    for copy in copies:
        copy.wait()
    for copy in far.values():
        copy.wait_send()
    for copy in near.values():
        copy.wait_send()
        copy.wait_recv()


def gather_tokens(own):
    devices = lax.axis_size("seq")
    parts, rows, width = own.shape
    vmem = pl.BlockSpec(memory_space=pltpu.VMEM)
    return pl.pallas_call(
        functools.partial(gather_tokens_kernel, devices),
        name="gather_tokens",
        out_shape=jax.ShapeDtypeStruct((parts, devices * rows, width), own.dtype),
        in_specs=[vmem],
        out_specs=vmem,
        scratch_shapes=[pltpu.SemaphoreType.DMA((parts, devices // 2))] * 4
        + [pltpu.SemaphoreType.DMA((parts,))],
        compiler_params=pltpu.CompilerParams(
            collective_id=0, has_side_effects=True, vmem_limit_bytes=16 * 1024 * 1024
        ),
    )(own)


def exchange_kernel(heads, segments, chunks, onward, *refs):
    if onward:
        terms_ref, residual_ref, stream_ref, result_ref, whole_ref = refs[:5]
        slots, total, sum_sends, sum_recvs, copy_sends, copy_recvs, hop_sends, hop_recvs, own_sem = refs[5:]
    else:
        terms_ref, residual_ref, result_ref, slots, total, sum_sends, sum_recvs = refs
    me = lax.axis_index("head")
    segment = lax.axis_index("segment")
    rows, width = residual_ref.shape
    piece = rows // chunks
    has_left, has_right = me >= 1, me + 1 < heads
    barrier = pltpu.get_barrier_semaphore()
    awaited = has_left.astype(jnp.int32) + has_right.astype(jnp.int32)

    @pl.when(has_left)
    def _():
        signal(barrier, {"head": me - 1})

    @pl.when(has_right)
    def _():
        signal(barrier, {"head": me + 1})

    if onward:
        awaited = awaited + (segment + 1 < segments).astype(jnp.int32)

        @pl.when(segment >= 1)
        def _():
            signal(barrier, {"segment": segment - 1})

    pl.semaphore_wait(barrier, awaited)

    def rows_of(chunk):
        return pl.ds(chunk * piece, piece)

    def within(position):
        return (position >= 0) & (position < heads)

    sides = ((0, 1), (1, -1))

    def sum_copy(side, sign, distance, chunk, first):
        source = (
            terms_ref.at[me + sign * distance, rows_of(chunk), :]
            if first
            else slots.at[side, distance, rows_of(chunk), :]
        )
        return remote(
            source,
            slots.at[side, distance - 1, rows_of(chunk), :],
            sum_sends.at[side, distance, chunk],
            sum_recvs.at[side, distance - 1, chunk],
            {"head": me + sign},
        )

    def sum_arrival(side, sign, distance, chunk):
        return remote(
            slots.at[side, distance, rows_of(chunk), :],
            slots.at[side, distance, rows_of(chunk), :],
            sum_sends.at[side, distance, chunk],
            sum_recvs.at[side, distance, chunk],
            {"head": me - sign},
        )

    def send_sums(distance, chunk):
        for side, sign in sides:

            @pl.when(within(me + sign * distance) & jnp.logical_not(within(me - sign)))
            def _():
                sum_copy(side, sign, distance, chunk, True).start()

            if distance < heads - 1:

                @pl.when(within(me + sign * distance) & within(me - sign))
                def _():
                    sum_arrival(side, sign, distance, chunk).wait_recv()
                    here = rows_of(chunk)
                    slots[side, distance, here, :] = (
                        slots[side, distance, here, :].astype(jnp.float32)
                        + terms_ref[me + sign * distance, here, :].astype(jnp.float32)
                    ).astype(jnp.bfloat16)
                    sum_copy(side, sign, distance, chunk, False).start()

    def finish(chunk):
        here = rows_of(chunk)
        total[...] = residual_ref[here, :].astype(jnp.float32) + terms_ref[me, here, :].astype(
            jnp.float32
        )
        for side, sign in sides:

            @pl.when(within(me - sign))
            def _():
                sum_arrival(side, sign, 0, chunk).wait_recv()
                total[...] += slots[side, 0, here, :].astype(jnp.float32)

        result_ref[here, :] = total[...].astype(jnp.bfloat16)
        if onward:

            @pl.when(segment + 1 < segments)
            def _():
                hop(chunk).start()

    def place(origin, chunk):
        return whole_ref.at[
            rows_of(chunk), pl.ds(pl.multiple_of(origin * width, width), width)
        ]

    def hop(chunk):
        return remote(
            result_ref.at[rows_of(chunk), :],
            place(me, chunk),
            hop_sends.at[chunk],
            hop_recvs.at[chunk],
            {"segment": segment + 1},
        )

    def hop_arrival(chunk):
        return remote(
            place(me, chunk),
            place(me, chunk),
            hop_sends.at[chunk],
            hop_recvs.at[chunk],
            {"segment": segment - 1},
        )

    def block_copy(side, sign, step, chunk):
        origin = me - sign * step
        return remote(
            place(origin, chunk),
            place(origin, chunk),
            copy_sends.at[side, step, chunk],
            copy_recvs.at[side, step, chunk],
            {"head": me + sign},
        )

    def block_arrival(side, sign, step, chunk):
        origin = me - sign * (step + 1)
        return remote(
            place(origin, chunk),
            place(origin, chunk),
            copy_sends.at[side, step, chunk],
            copy_recvs.at[side, step, chunk],
            {"head": me - sign},
        )

    def send_blocks(step, chunk):
        if step == 0:

            @pl.when(segment >= 1)
            def _():
                hop_arrival(chunk).wait_recv()

        for side, sign in sides:
            if step > 0:

                @pl.when(within(me - sign * step))
                def _():
                    block_arrival(side, sign, step - 1, chunk).wait_recv()

            if step < heads - 1:

                @pl.when(within(me - sign * step) & within(me + sign))
                def _():
                    block_copy(side, sign, step, chunk).start()

    if onward:
        own = pltpu.make_async_copy(
            stream_ref, whole_ref.at[:, pl.ds(pl.multiple_of(me * width, width), width)], own_sem
        )

        @pl.when(segment == 0)
        def _():
            own.start()
            own.wait()

    stages = [functools.partial(send_sums, distance) for distance in range(heads - 1, 0, -1)]
    stages.append(finish)
    if onward:
        stages += [functools.partial(send_blocks, step) for step in range(heads)]
    for moment in range(chunks + len(stages) - 1):
        for index, stage in enumerate(stages):
            if 0 <= moment - index < chunks:
                stage(moment - index)

    for chunk in range(chunks):
        for side, sign in sides:
            for distance in range(1, heads):

                @pl.when(within(me + sign * distance))
                def _():
                    sum_copy(side, sign, distance, chunk, True).wait_send()

            if onward:
                for step in range(heads - 1):

                    @pl.when(within(me - sign * step) & within(me + sign))
                    def _():
                        block_copy(side, sign, step, chunk).wait_send()

        if onward:

            @pl.when(segment + 1 < segments)
            def _():
                hop(chunk).wait_send()


def exchange(terms, residual, following):
    heads, rows, width = terms.shape
    segments = lax.axis_size("segment")
    onward = following is not None
    chunks = 4
    vmem = pl.BlockSpec(memory_space=pltpu.VMEM)
    shapes = [jax.ShapeDtypeStruct((rows, width), jnp.bfloat16)]
    scratch = [
        pltpu.VMEM((2, heads, rows, width), jnp.bfloat16),
        pltpu.VMEM((rows // chunks, width), jnp.float32),
    ] + [pltpu.SemaphoreType.DMA((2, heads, chunks))] * 2
    operands = [terms, residual]
    if onward:
        operands.append(following)
        shapes.append(jax.ShapeDtypeStruct((rows, heads * width), jnp.bfloat16))
        scratch += [pltpu.SemaphoreType.DMA((2, heads, chunks))] * 2
        scratch += [pltpu.SemaphoreType.DMA((chunks,))] * 2 + [pltpu.SemaphoreType.DMA]
    return pl.pallas_call(
        functools.partial(exchange_kernel, heads, segments, chunks, onward),
        name="exchange" if onward else "reduce",
        out_shape=tuple(shapes),
        in_specs=[vmem] * len(operands),
        out_specs=(vmem,) * len(shapes),
        scratch_shapes=scratch,
        compiler_params=pltpu.CompilerParams(
            collective_id=1 if onward else 2,
            has_side_effects=True,
            vmem_limit_bytes=24 * 1024 * 1024,
        ),
    )(*operands)


def gather_heads(block):
    heads = lax.axis_size("head")
    spread = jnp.broadcast_to(block[None], (heads,) + block.shape)
    return lax.all_to_all(spread, "head", split_axis=0, concat_axis=0, tiled=True)


def run_section(
    whole, gain_row, qkv_matrix, head_gains, rate_row, out_gain_row, out_weights, fasts, norms, active
):
    rows = whole.shape[0]
    heads = lax.axis_size("head")
    head_width = head_gains.shape[-1]
    normed = (rms_scale(whole.astype(jnp.float32)) * gain_row).astype(jnp.bfloat16)
    projected = dot(normed, qkv_matrix).reshape(rows, 3, head_width)
    queries = (rms_scale(projected[:, 0]) * head_gains[0]).astype(jnp.bfloat16)
    key_rows = (rms_scale(projected[:, 1]) * head_gains[1]).astype(jnp.bfloat16)
    out_grad = (-rate_row[:, None] * projected[:, 2]).astype(jnp.bfloat16)
    both = gather_tokens(jnp.stack([key_rows, out_grad]))
    return fast_step(active, both, queries, fasts, norms, out_gain_row, out_weights, heads)


def shards(stream, in_gain, w_qkv, qk_gain, w_one, w_three, w_two, token_rate, out_gain, w_out):
    segment_index = lax.axis_index("segment")
    span_count = stream.shape[0]
    moments = span_count + lax.axis_size("segment") - 1
    qkv_matrix = w_qkv[0].reshape(w_qkv.shape[1], -1)
    fasts = (
        w_one[0, 0].astype(jnp.float32),
        w_three[0, 0].astype(jnp.float32),
        w_two[0, 0].astype(jnp.float32).T,
    )
    norms = (
        jnp.stack([jnp.sqrt(jnp.sum(matrix * matrix, axis=0, keepdims=True)) for matrix in fasts[:2]]),
        jnp.sqrt(jnp.sum(fasts[2] * fasts[2], axis=1, keepdims=True)),
    )
    collected = jnp.zeros(stream.shape, jnp.bfloat16)
    source = stream[0]
    whole = gather_heads(source).swapaxes(0, 1).reshape(source.shape[0], -1)
    for moment in range(moments):
        span_index = moment - segment_index
        active = (span_index >= 0) & (span_index < span_count)
        clipped = jnp.clip(span_index, 0, span_count - 1)
        rate_row = lax.dynamic_index_in_dim(token_rate[0], clipped, 0, keepdims=False)
        terms, *fasts = run_section(
            whole,
            in_gain[0],
            qkv_matrix,
            qk_gain[0, 0],
            rate_row,
            out_gain[0, :1],
            w_out[0, 0],
            fasts,
            norms,
            active.astype(jnp.int32)[None],
        )
        if moment + 1 < moments:
            following = stream[min(moment + 1, span_count - 1)]
            result, whole = exchange(terms, source, following)
            source = lax.dynamic_slice_in_dim(
                whole, lax.axis_index("head") * source.shape[1], source.shape[1], axis=1
            )
        else:
            (result,) = exchange(terms, source, None)
        chosen = jnp.arange(span_count) == span_index
        collected = jnp.where(chosen[:, None, None], result[None], collected)
    return collected[None]


def solution(mesh):
    placed = (
        P(None, "seq", "head"),
        P("segment", None),
        P("segment", None, "head", None, None),
        P("segment", "head", None, None),
        P("segment", "head", None, None),
        P("segment", "head", None, None),
        P("segment", "head", None, None),
        P("segment", None, "seq"),
        P("segment", "head", None),
        P("segment", "head", None, None),
    )
    return jax.shard_map(
        shards,
        mesh=mesh,
        in_specs=placed,
        out_specs=P("segment", None, "seq", "head"),
        check_vma=False,
    )
```
